32 devices in a mesh: rows: 8 (over z, x), chan: 4 (over y, core).
Axes of the slice: x: 2, y: 2, z: 4, core: 2. Of those that a mesh axis runs over, the one named last changes fastest.
Arguments:
- frames: bfloat16 [9, 32, 480, 256], P(None, 'rows', 'chan'), may hold values from -450 to 450
- spatial_weight: bfloat16 [256, 2304], P('rows'), may hold values from -0.125 to 0.125
- temporal_weight: bfloat16 [256, 768], P('rows'), may hold values from -0.21875 to 0.21875
- down_weight: bfloat16 [256, 2304], P('rows'), may hold values from -0.125 to 0.125
- norm_gain: float32 [256], replicated, may hold values from 0.5 to 1.5
- norm_shift: float32 [256], replicated, may hold values from -3 to 3
- down_bias: float32 [256], replicated, may hold values from -3 to 3
Outputs:
- latent: bfloat16 [9, 16, 240, 256], P(None, 'rows', 'chan')
The draws below stay inside these ranges and needn't reach their ends.
All inputs are finite; a program needn't handle non-finite values.
Results may differ from the reference program's by a relative error of at most 0.0053.
Values may be sent and summed in bfloat16 or wider, within the bound.
No kernel may reach another device: no remote copies, remote signals or barrier semaphores. Data moves between devices by JAX's collectives and lax.ppermute only.
A program may use at most 128 MiB of HBM per device.

```python
import math
import jax
import jax.numpy as jnp
from jax import lax

FEATURE_CHANNELS = 256
WIDTH = 480
FRAMES = 9
GROUPS = 32
HEIGHT = 32


def draw_frames(key, part):
    value_key, row_key, col_key = jax.random.split(key, 3)
    frame_key = jax.random.fold_in(key, 11)
    offset_key = jax.random.fold_in(key, 12)
    spike_random_key = jax.random.fold_in(key, 13)
    extent_random_key = jax.random.fold_in(key, 14)
    layout_random_key = jax.random.fold_in(key, 15)
    polarity_key = jax.random.fold_in(key, 16)
    full_shape = (FRAMES, HEIGHT, WIDTH, FEATURE_CHANNELS)
    location_shape = (FRAMES, HEIGHT, WIDTH)
    row_place = jnp.arange(HEIGHT, dtype=jnp.float32) / max(HEIGHT - 1, 1)
    row_scale = jnp.exp(jax.random.uniform(row_key, (HEIGHT,), dtype=jnp.float32) * math.log(10.0 / 3.0)) * jnp.exp(row_place * math.log(3.0))
    col_scale = jnp.exp(jax.random.uniform(col_key, (WIDTH,), dtype=jnp.float32) * math.log(10.0))
    values = jnp.clip(jax.random.normal(value_key, full_shape, dtype=jnp.float32), -4.0, 4.0)
    rescaled_values = 0.04 * values * row_scale[None, :, None, None] * col_scale[None, None, :, None]
    frame_factor = jax.random.uniform(frame_key, (FRAMES,), dtype=jnp.float32, minval=0.0, maxval=2.0)
    chan_offset = 0.8 * jnp.clip(jax.random.normal(offset_key, (FEATURE_CHANNELS,), dtype=jnp.float32), -3.0, 3.0)
    rescaled_values = rescaled_values + frame_factor[:, None, None, None] * chan_offset[None, None, None, :]
    spike_mask = jax.random.bernoulli(spike_random_key, 6e-05, location_shape).astype(jnp.float32)
    spike_polarity = 2.0 * jax.random.bernoulli(polarity_key, 0.5, location_shape).astype(jnp.float32) - 1.0
    spike_extent = jax.random.uniform(extent_random_key, location_shape, dtype=jnp.float32, minval=320.0, maxval=420.0)
    spike_layout_values = jax.random.uniform(layout_random_key, (FEATURE_CHANNELS,), dtype=jnp.float32, minval=-1.0, maxval=1.0)
    spike_magnitude = spike_mask * spike_polarity * spike_extent
    rescaled_values = rescaled_values + spike_magnitude[:, :, :, None] * spike_layout_values[None, None, None, :]
    return jnp.clip(rescaled_values, -449.0, 449.0).astype(jnp.bfloat16)


def shard_levels(stream_key, dims, cuts, low, high):
    def one(dim, shards_of):
        heights = jax.random.uniform(jax.random.fold_in(jax.random.fold_in(stream_key, 6), dim), (shards_of,), jnp.float32, low / len(cuts), high / len(cuts))
        return jnp.repeat(jnp.exp(heights), dims[dim] // shards_of).reshape((-1,) + (1,) * (len(dims) - dim - 1))

    level = one(*cuts[0])
    for cut in cuts[1:]:
        level = level * one(*cut)
    return level


def normal_values(rng, extent, deviation, reach, cuts=(), kind=jnp.bfloat16):
    array = jax.random.normal(rng, extent, jnp.float32) * deviation
    if len(cuts) > 0:
        array = shard_levels(rng, extent, cuts, -0.22, 0.18) * array
    return jnp.clip(array, min=-reach, max=reach).astype(kind)


def setup_inputs(seed: int = 0) -> dict:
    seeds = jax.random.split(jax.random.key(seed), 8)
    return {
        "frames": draw_frames(jax.random.fold_in(seeds[7], 71), 0),
        "spatial_weight": normal_values(seeds[1], (FEATURE_CHANNELS, 9 * FEATURE_CHANNELS), (9 * FEATURE_CHANNELS) ** -0.5, 0.125, ((0, 8),)),
        "temporal_weight": normal_values(seeds[2], (FEATURE_CHANNELS, 3 * FEATURE_CHANNELS), (3 * FEATURE_CHANNELS) ** -0.5, 0.21875, ((0, 8),)),
        "down_weight": normal_values(seeds[3], (FEATURE_CHANNELS, 9 * FEATURE_CHANNELS), (9 * FEATURE_CHANNELS) ** -0.5, 0.125, ((0, 8),)),
        "norm_gain": jnp.clip(jax.random.uniform(seeds[4], (FEATURE_CHANNELS,), jnp.float32, 0.5, 1.5), 0.5, 1.5),
        "norm_shift": normal_values(seeds[5], (FEATURE_CHANNELS,), 0.5, 3.0, (), jnp.float32),
        "down_bias": normal_values(seeds[6], (FEATURE_CHANNELS,), 0.5, 3.0, (), jnp.float32),
    }


epsilon = 1e-06

def spatial_frame(picture, weight_rows, channels):
    height_all = picture.shape[0]
    width_all = picture.shape[1]
    padded = jnp.pad(picture, ((1, 1), (1, 1), (0, 0)))
    summed = jnp.zeros((height_all * width_all, channels), jnp.float32)
    for tap_index in range(9):
        row_offset = tap_index // 3
        col_offset = tap_index % 3
        window = padded[row_offset:row_offset + height_all, col_offset:col_offset + width_all].reshape(height_all * width_all, channels)
        summed = summed + jnp.dot(window, weight_rows[:, tap_index * channels:(tap_index + 1) * channels], preferred_element_type=jnp.float32)
    return summed.reshape(height_all, width_all, channels)

def temporal_frame(first, frame_index, weight_rows, channels):
    summed = None
    for tap_index in range(3):
        source = jnp.maximum(frame_index - 2 + tap_index, 0).astype(jnp.int32)
        picture = lax.dynamic_index_in_dim(first, source, 0, keepdims=False)
        flattened = picture.reshape(-1, channels)
        product = jnp.dot(flattened, weight_rows[:, tap_index * channels:(tap_index + 1) * channels], preferred_element_type=jnp.float32)
        summed = product if summed is None else summed + product
    return summed.reshape(first.shape[1], first.shape[2], channels)

def down_frame(picture, weight_rows, channels):
    rows_out = picture.shape[0] // 2
    cols_out = picture.shape[1] // 2
    padded = jnp.pad(picture, ((0, 1), (0, 1), (0, 0)))
    summed = jnp.zeros((rows_out * cols_out, channels), jnp.float32)
    for tap_index in range(9):
        row_offset = tap_index // 3
        col_offset = tap_index % 3
        window = padded[row_offset:row_offset + 2 * rows_out:2, col_offset:col_offset + 2 * cols_out:2].reshape(rows_out * cols_out, channels)
        summed = summed + jnp.dot(window, weight_rows[:, tap_index * channels:(tap_index + 1) * channels], preferred_element_type=jnp.float32)
    return summed.reshape(rows_out, cols_out, channels)

def reference(frames, spatial_weight, temporal_weight, down_weight, norm_gain, norm_shift, down_bias):
    channels = frames.shape[3]
    group_width = channels // GROUPS
    frame_count = frames.shape[0]
    cell_count = frame_count * frames.shape[1] * frames.shape[2] * group_width

    def spatial_step(picture):
        return spatial_frame(picture, spatial_weight, channels).astype(jnp.bfloat16)
    first = lax.map(spatial_step, frames)
    frame_order = jnp.arange(frame_count, dtype=jnp.int32)

    def temporal_step(frame_index):
        return temporal_frame(first, frame_index, temporal_weight, channels)
    hidden = lax.map(temporal_step, frame_order)
    channel_sums = lax.optimization_barrier(jnp.sum(hidden, axis=(0, 1, 2)))
    means = channel_sums.reshape(GROUPS, group_width).sum(axis=1) / cell_count
    chan_mean = jnp.repeat(means, group_width)
    centered = hidden - chan_mean
    spread = lax.optimization_barrier(jnp.sum(centered * centered, axis=(0, 1, 2)))
    variance = spread.reshape(GROUPS, group_width).sum(axis=1) / cell_count
    chan_var = jnp.repeat(variance, group_width)
    rescaled_values = lax.rsqrt(chan_var + epsilon)

    def latent_step(frame_index):
        hidden_frame = lax.dynamic_index_in_dim(hidden, frame_index, 0, keepdims=False)
        act = jax.nn.silu((hidden_frame - chan_mean) * rescaled_values * norm_gain + norm_shift).astype(jnp.bfloat16)
        return (down_frame(act, down_weight, channels) + down_bias).astype(jnp.bfloat16)
    return lax.map(latent_step, frame_order)
```

```python
import functools

import jax
import jax.numpy as jnp
from jax import lax
from jax.experimental import pallas as pl
from jax.experimental.pallas import tpu as pltpu
from jax.sharding import PartitionSpec as P

GROUPS = 32
EPSILON = 1e-06
LANE_COLS = 128
F32 = jnp.float32
BF16 = jnp.bfloat16


def shifted(block, axis, distance):
    count = lax.axis_size(axis)
    route = [(i, i + distance) for i in range(count) if 0 <= i + distance < count]
    return lax.ppermute(block, axis, route)


def swapped(block, axis, bit):
    return lax.ppermute(block, axis, [(i, i ^ bit) for i in range(lax.axis_size(axis))])


def weight_parts(weight):
    chan = lax.axis_size("chan")
    part = weight.shape[0] // chan
    own = lax.dynamic_slice_in_dim(weight, lax.axis_index("chan") * part, part, 0)
    return own


def spread_rows(own):
    rows = lax.axis_size("rows")
    return lax.all_to_all(jnp.broadcast_to(own[None], (rows,) + own.shape), "rows", 0, 0)


def spread_chan(held):
    parts = [held]
    bit = lax.axis_size("chan") // 2
    while bit:
        parts = parts + [swapped(part, "chan", bit) for part in parts]
        bit //= 2
    order = [0]
    bit = lax.axis_size("chan") // 2
    while bit:
        order = order + [o ^ bit for o in order]
        bit //= 2
    return [parts[order.index(k)] for k in range(len(order))]


def assemble(chan_index, parts, wide, weight):
    for k, part in enumerate(parts):
        wide[:, chan_index ^ k] = part[...].astype(F32)
    weight[...] = wide[...].reshape(weight.shape).astype(BF16)


def front_kernel(
    index, frames, top, bottom, pack, pack_top, pack_bottom, *rest, parts, channels, n_frames
):
    part_refs = rest[:parts]
    first_row, hidden, stats, temporal, wide, weight, x, held, moments = rest[parts:]
    step = pl.program_id(0)
    rows, cols = frames.shape[1], frames.shape[2]

    @pl.when(step == 0)
    def _():
        assemble(index[1], part_refs, wide, weight)
        temporal[...] = weight[:, 9 * channels :]

    def joined(main, side):
        return jnp.concatenate([main.astype(F32), side.astype(F32)], axis=1).astype(BF16)

    x[0] = joined(top[0], pack_top[0])[0]
    x[1 : rows + 1] = joined(frames[0], pack[0])
    x[rows + 1] = joined(bottom[0], pack_bottom[0])[0]
    size = rows * LANE_COLS
    products = []
    for b in range(3):
        total = None
        for a in range(3):
            tap = 3 * a + b
            lhs = x[a : a + rows].reshape(size, channels)
            term = jnp.dot(
                lhs,
                weight[:, tap * channels : (tap + 1) * channels],
                preferred_element_type=F32,
            )
            total = term if total is None else total + term
        products.append(total.reshape(rows, LANE_COLS, channels))
    first = (
        products[1]
        + pltpu.roll(products[0], 1, 1)
        + pltpu.roll(products[2], LANE_COLS - 1, 1)
    )
    first = first.astype(BF16)
    first_row[0] = first[0]
    first = first.reshape(size, channels)

    @pl.when(step == 0)
    def _():
        held[0] = first
        held[1] = first

    slot = lax.rem(step, 2)
    base = 9 * channels
    total = (
        jnp.dot(held[slot], weight[:, base : base + channels], preferred_element_type=F32)
        + jnp.dot(
            held[1 - slot],
            weight[:, base + channels : base + 2 * channels],
            preferred_element_type=F32,
        )
        + jnp.dot(first, weight[:, base + 2 * channels :], preferred_element_type=F32)
    )
    held[slot] = first
    total = total.reshape(rows, LANE_COLS, channels)
    for k in range(channels // 128):
        hidden[0, :, k] = total[:, :, k * 128 : (k + 1) * 128]
    inner = total[:, :cols].reshape(rows * cols, channels)
    count = float(rows * cols)
    mean = jnp.sum(inner, axis=0, keepdims=True) / count
    spread = jnp.sum(jnp.square(inner - mean), axis=0, keepdims=True)

    @pl.when(step == 0)
    def _():
        moments[0:1] = mean
        moments[1:2] = spread

    @pl.when(step > 0)
    def _():
        done = step.astype(F32)
        delta = mean - moments[0:1]
        moments[0:1] = moments[0:1] + delta / (done + 1.0)
        moments[1:2] = moments[1:2] + spread + delta * delta * (count * done / (done + 1.0))

    @pl.when(step == n_frames - 1)
    def _():
        stats[...] = jnp.broadcast_to(moments[0:2][None], stats.shape)


def back_kernel(
    index, hidden, halo, temporal, stats, gain, shift, bias, *rest, parts, channels, count
):
    part_refs = rest[:parts]
    latent, wide, weight, affine, full, even, odd = rest[parts:]
    step = pl.program_id(0)
    batch, rows = hidden.shape[0], hidden.shape[1]
    half = LANE_COLS // 2
    cols_out = latent.shape[2]
    rows_out = rows // 2
    blocks = channels // 128

    @pl.when(step == 0)
    def _():
        assemble(index[1], part_refs, wide, weight)
        devices = stats.shape[0]
        group = channels // GROUPS
        means = stats[:, 0]
        mean = jnp.sum(means, axis=0, keepdims=True) / float(devices)
        spread = jnp.sum(stats[:, 1], axis=0, keepdims=True) + count * jnp.sum(
            jnp.square(means - mean), axis=0, keepdims=True
        )
        lane = lax.broadcasted_iota(jnp.int32, (channels, channels), 0) // group
        same = lane == lax.broadcasted_iota(jnp.int32, (channels, channels), 1) // group
        same = same.astype(F32)

        def over_group(values):
            return jnp.dot(
                jnp.broadcast_to(values, (8, channels)),
                same,
                precision=lax.Precision.HIGHEST,
                preferred_element_type=F32,
            )[0:1] / float(group)

        group_mean = over_group(mean)
        total = over_group(spread / (count * devices) + jnp.square(mean - group_mean))
        affine[0:1] = group_mean
        affine[1:2] = lax.rsqrt(total + EPSILON)

    mean = affine[0:1]
    rstd = affine[1:2]
    for i in range(batch):
        frame = step * batch + i
        older = jnp.maximum(frame - 2, 0)
        old = jnp.maximum(frame - 1, 0)
        extra = (
            jnp.dot(halo[older], temporal[:, :channels], preferred_element_type=F32)
            + jnp.dot(
                halo[old], temporal[:, channels : 2 * channels], preferred_element_type=F32
            )
            + jnp.dot(halo[frame], temporal[:, 2 * channels :], preferred_element_type=F32)
        )
        for k in range(blocks):
            full[i, k] = extra[:, k * 128 : (k + 1) * 128]

    def columns(i, row, start):
        picked = pl.ds(start, half, stride=2)
        return jnp.concatenate(
            [
                hidden[i, row, k, picked] if row < rows else full[i, k, picked]
                for k in range(blocks)
            ],
            axis=1,
        )

    def activated(values):
        return jax.nn.silu((values - mean) * rstd * gain[...] + shift[...])

    for i in range(batch):
        for row in range(rows + 1):
            place = row // 2 if row % 2 == 0 else rows_out + 1 + row // 2
            e = activated(columns(i, row, 0))
            o = activated(columns(i, row, 1))
            at = lax.broadcasted_iota(jnp.int32, e.shape, 0)
            keep = (index[3] == 0) | (at < cols_out)
            if row == rows:
                keep = keep & (index[2] == 0)
                o = jnp.where(index[2] == 0, o, 0.0)
            e = jnp.where(keep, e, 0.0)
            even[place, i] = e.astype(BF16)
            odd[place, i] = o.astype(BF16)
    size = rows_out * batch * half
    starts = (0, rows_out + 1, 1)
    sums = []
    for source, taps in ((even, (0,)), (odd, (1,)), (even, (2,))):
        total = None
        for a in range(3):
            lhs = source[starts[a] : starts[a] + rows_out].reshape(size, channels)
            tap = 3 * a + taps[0]
            term = jnp.dot(
                lhs,
                weight[:, tap * channels : (tap + 1) * channels],
                preferred_element_type=F32,
            )
            total = term if total is None else total + term
        sums.append(total.reshape(rows_out * batch, half, channels))
    out = sums[0] + sums[1] + pltpu.roll(sums[2], half - 1, 1) + bias[...]
    out = out.reshape(rows_out, batch, half, channels).astype(BF16)
    for p in range(rows_out):
        for i in range(batch):
            latent[i, p] = out[p, i, :cols_out]


def whole(shape):
    return pl.BlockSpec(shape, lambda i, *_: (0,) * len(shape))


def gathered_parts(weight):
    chan = lax.axis_size("chan")
    if weight.shape[0] % (8 * chan) == 0:
        own = weight_parts(weight)
        return own, True
    return lax.all_gather(weight, "rows", axis=0, tiled=True), False


def per_device(
    frames, spatial_weight, temporal_weight, down_weight, norm_gain, norm_shift, down_bias
):
    n_frames, rows, cols, channels = frames.shape
    row_devices, chan_devices = lax.axis_size("rows"), lax.axis_size("chan")
    row_index, chan_index = lax.axis_index("rows"), lax.axis_index("chan")
    index = jnp.stack(
        [
            row_index,
            chan_index,
            (row_index == row_devices - 1).astype(jnp.int32),
            (chan_index == chan_devices - 1).astype(jnp.int32),
        ]
    ).astype(jnp.int32)

    top = shifted(frames[:, rows - 1 :], "rows", 1)
    bottom = shifted(frames[:, :1], "rows", -1)
    right = shifted(frames[:, :, :8], "chan", -1)
    left = shifted(frames[:, :, cols - 8 :], "chan", 1)
    at = lax.broadcasted_iota(jnp.int32, right.shape, 2)
    pack = jnp.where(at == 7, left, right)
    pack_top = shifted(pack[:, rows - 1 :], "rows", 1)
    pack_bottom = shifted(pack[:, :1], "rows", -1)

    split = spatial_weight.shape[0] % (8 * chan_devices) == 0
    if split:
        own = jnp.concatenate([weight_parts(spatial_weight), weight_parts(temporal_weight)], 1)
        front_parts = spread_chan(spread_rows(own))
        back_parts = spread_chan(
            lax.all_gather(weight_parts(down_weight), "rows", axis=0, tiled=False)
        )
    else:
        joint = jnp.concatenate([spatial_weight, temporal_weight], 1)
        front_parts = [lax.all_gather(joint, "rows", axis=0, tiled=True)]
        back_parts = [lax.all_gather(down_weight, "rows", axis=0, tiled=True)]
        front_parts = [front_parts[0].reshape(channels // 8, 8, -1)]
        back_parts = [back_parts[0].reshape(channels // 8, 8, -1)]
        index = index.at[1].set(0)
    parts = len(front_parts)
    piece = front_parts[0].shape
    wide_front = (piece[0], parts, piece[1], piece[2])
    piece_back = back_parts[0].shape
    wide_back = (piece_back[0], parts, piece_back[1], piece_back[2])

    frame_block = lambda *tail: pl.BlockSpec((1,) + tail, lambda i, *_: (i,) + (0,) * len(tail))
    flops = 2 * n_frames * rows * LANE_COLS * channels * channels
    first_row, hidden, stats, temporal = pl.pallas_call(
        functools.partial(front_kernel, parts=parts, channels=channels, n_frames=n_frames),
        grid_spec=pltpu.PrefetchScalarGridSpec(
            num_scalar_prefetch=1,
            grid=(n_frames,),
            in_specs=[
                frame_block(rows, cols, channels),
                frame_block(1, cols, channels),
                frame_block(1, cols, channels),
                frame_block(rows, 8, channels),
                frame_block(1, 8, channels),
                frame_block(1, 8, channels),
            ]
            + [whole(piece)] * parts,
            out_specs=[
                frame_block(LANE_COLS, channels),
                frame_block(rows, channels // 128, LANE_COLS, 128),
                whole((row_devices * chan_devices, 2, channels)),
                whole((channels, 3 * channels)),
            ],
            scratch_shapes=[
                pltpu.VMEM(wide_front, F32),
                pltpu.VMEM((channels, 12 * channels), BF16),
                pltpu.VMEM((rows + 2, LANE_COLS, channels), BF16),
                pltpu.VMEM((2, rows * LANE_COLS, channels), BF16),
                pltpu.VMEM((8, channels), F32),
            ],
        ),
        out_shape=[
            jax.ShapeDtypeStruct((n_frames, LANE_COLS, channels), BF16),
            jax.ShapeDtypeStruct((n_frames, rows, channels // 128, LANE_COLS, 128), F32),
            jax.ShapeDtypeStruct((row_devices * chan_devices, 2, channels), F32),
            jax.ShapeDtypeStruct((channels, 3 * channels), BF16),
        ],
        compiler_params=pltpu.CompilerParams(
            dimension_semantics=("arbitrary",), vmem_limit_bytes=40 << 20
        ),
        cost_estimate=pl.CostEstimate(
            flops=12 * flops, bytes_accessed=12 << 20, transcendentals=0
        ),
        name="front",
    )(index, frames, top, bottom, pack, pack_top, pack_bottom, *front_parts)

    halo = shifted(first_row, "rows", -1)
    all_stats = lax.all_to_all(stats, ("rows", "chan"), 0, 0)

    batch = 3 if n_frames % 3 == 0 else 1
    vector = lambda v: v.reshape(1, channels)
    rows_out, cols_out = rows // 2, cols // 2
    batch_block = lambda *tail: pl.BlockSpec(
        (batch,) + tail, lambda i, *_: (i,) + (0,) * len(tail)
    )
    return pl.pallas_call(
        functools.partial(
            back_kernel, parts=parts, channels=channels, count=float(n_frames * rows * cols)
        ),
        grid_spec=pltpu.PrefetchScalarGridSpec(
            num_scalar_prefetch=1,
            grid=(n_frames // batch,),
            in_specs=[
                batch_block(rows, channels // 128, LANE_COLS, 128),
                whole((n_frames, LANE_COLS, channels)),
                whole((channels, 3 * channels)),
                whole(all_stats.shape),
                whole((1, channels)),
                whole((1, channels)),
                whole((1, channels)),
            ]
            + [whole(piece_back)] * parts,
            out_specs=batch_block(rows_out, cols_out, channels),
            scratch_shapes=[
                pltpu.VMEM(wide_back, F32),
                pltpu.VMEM((channels, 9 * channels), BF16),
                pltpu.VMEM((8, channels), F32),
                pltpu.VMEM((batch, channels // 128, LANE_COLS, 128), F32),
                pltpu.VMEM((rows + 1, batch, LANE_COLS // 2, channels), BF16),
                pltpu.VMEM((rows + 1, batch, LANE_COLS // 2, channels), BF16),
            ],
        ),
        out_shape=jax.ShapeDtypeStruct((n_frames, rows_out, cols_out, channels), BF16),
        compiler_params=pltpu.CompilerParams(
            dimension_semantics=("arbitrary",), vmem_limit_bytes=40 << 20
        ),
        cost_estimate=pl.CostEstimate(
            flops=3 * flops, bytes_accessed=10 << 20, transcendentals=4 << 20
        ),
        name="back",
    )(
        index,
        hidden,
        halo,
        temporal,
        all_stats,
        vector(norm_gain),
        vector(norm_shift),
        vector(down_bias),
        *back_parts,
    )


def solution(mesh):
    placed = (
        P(None, "rows", "chan", None),
        P("rows", None),
        P("rows", None),
        P("rows", None),
        P(),
        P(),
        P(),
    )
    return jax.shard_map(
        per_device,
        mesh=mesh,
        in_specs=placed,
        out_specs=P(None, "rows", "chan", None),
        check_vma=False,
    )
```

```python
import functools

import jax
import jax.numpy as jnp
from jax import lax
from jax.experimental import pallas as pl
from jax.experimental.pallas import tpu as pltpu
from jax.sharding import PartitionSpec as P

GROUPS = 32
EPSILON = 1e-06
LANE_COLS = 128
SIDE = 8
GRANT = 56
BATCH = 3
F32 = jnp.float32
BF16 = jnp.bfloat16


def shifted(block, axis, distance):
    count = lax.axis_size(axis)
    return lax.ppermute(block, axis, [(i, (i + distance) % count) for i in range(count)])


def swapped(block, axis, bit):
    return lax.ppermute(block, axis, [(i, i ^ bit) for i in range(lax.axis_size(axis))])


def spread_chan(held):
    parts = {0: held}
    bit = lax.axis_size("chan") // 2
    while bit:
        parts.update({k ^ bit: swapped(part, "chan", bit) for k, part in parts.items()})
        bit //= 2
    return [parts[k] for k in range(len(parts))]


def anywhere(count):
    return [pl.BlockSpec(memory_space=pl.ANY)] * count


def staged_call(body, sources, kept, outs, sems, name):
    return pl.pallas_call(
        body,
        out_shape=outs,
        in_specs=[pl.BlockSpec(memory_space=pltpu.HBM)] * len(sources),
        out_specs=anywhere(len(outs)),
        scratch_shapes=[pltpu.VMEM(k.shape, k.dtype) for k in kept]
        + [pltpu.SemaphoreType.DMA((n,)) for n in sems],
        compiler_params=params(GRANT, grid=0),
        name=name,
    )(*sources)


def side_columns(frames):
    n_frames, rows, cols, channels = frames.shape
    side = jax.ShapeDtypeStruct((n_frames, rows, SIDE, channels), frames.dtype)

    def body(source, first, last, first_kept, last_kept, sems, out_sems):
        moves = [
            (source.at[:, :, 0:SIDE], first_kept, first),
            (source.at[:, :, cols - SIDE :], last_kept, last),
        ]
        fetches = [
            pltpu.make_async_copy(src, hold, sems.at[k])
            for k, (src, hold, _) in enumerate(moves)
        ]
        stores = [
            pltpu.make_async_copy(hold, dst, out_sems.at[k])
            for k, (_, hold, dst) in enumerate(moves)
        ]
        for fetch in fetches:
            fetch.start()
        for fetch, store in zip(fetches, stores):
            fetch.wait()
            store.start()
        for store in stores:
            store.wait()

    return staged_call(body, [frames], [side, side], [side, side], (2, 2), "side_columns")


def weight_pieces(spatial, temporal, down, channels, copies, part):
    width = 3 * channels
    depth = spatial.shape[0]
    tap = jax.ShapeDtypeStruct((depth, width), spatial.dtype)
    own = jax.ShapeDtypeStruct((part, down.shape[1]), down.dtype)
    picks = [
        (n, at) for n, w in enumerate((spatial, temporal)) for at in range(0, w.shape[1], width)
    ]

    def body(*refs):
        taps, down_ref = refs[:2], refs[2]
        outs, kept, (sems, out_sems) = refs[3:5], refs[5:7], refs[7:]
        chan = lax.axis_index("chan")
        for k, (n, at) in enumerate(picks):
            @pl.when(chan == k)
            def _():
                pltpu.make_async_copy(
                    taps[n].at[:, at : at + width], kept[0], sems.at[0]
                ).start()
        rows = down_ref.at[pl.ds(pl.multiple_of(chan * part, part), part)]
        fetches = [
            pltpu.make_async_copy(taps[0].at[:, 0:width], kept[0], sems.at[0]),
            pltpu.make_async_copy(rows, kept[1], sems.at[1]),
        ]
        fetches[1].start()
        stores = []
        for k, fetch in enumerate(fetches):
            fetch.wait()
            for j in range(copies):
                store = pltpu.make_async_copy(
                    kept[k], outs[k].at[j], out_sems.at[len(stores)]
                )
                store.start()
                stores.append(store)
        for store in stores:
            store.wait()

    outs = [jax.ShapeDtypeStruct((copies,) + k.shape, k.dtype) for k in (tap, own)]
    return staged_call(
        body, [spatial, temporal, down], [tap, own], outs, (2, 2 * copies), "weight_pieces"
    )


def extended_kernel(last_row, first_row, left, right, low, high, pack):
    rows, cols = left.shape[1], last_row.shape[2]
    chan = lax.axis_index("chan")
    at = lax.broadcasted_iota(jnp.int32, left.shape, 2)
    before = jnp.where(chan == 0, 0.0, left[...].astype(F32))
    after = jnp.where(chan == lax.axis_size("chan") - 1, 0.0, right[...].astype(F32))
    side = jnp.where(at == SIDE - 1, before, after).astype(BF16)
    pack[...] = side
    low[:, :, :cols] = last_row[...]
    low[:, :, cols:] = side[:, rows - 1 :]
    high[:, :, :cols] = first_row[...]
    high[:, :, cols:] = side[:, :1]


def extended_call(frames, left, right):
    n_frames, rows, cols, channels = frames.shape
    row = (n_frames, 1, cols, channels)
    full = (n_frames, 1, LANE_COLS, channels)
    wide = jax.ShapeDtypeStruct(full, BF16)
    return pl.pallas_call(
        extended_kernel,
        grid=(1,),
        in_specs=[
            pl.BlockSpec(row, lambda i: (0, rows - 1, 0, 0)),
            pl.BlockSpec(row, lambda i: (0, 0, 0, 0)),
            whole(left.shape),
            whole(right.shape),
        ],
        out_specs=[whole(full), whole(full), whole(left.shape)],
        out_shape=[wide, wide, jax.ShapeDtypeStruct(left.shape, BF16)],
        compiler_params=params(16),
        cost_estimate=cost(0, 3),
        name="extended",
    )(frames, frames, left, right)


def repeated(own, copies):
    return jnp.broadcast_to(own[None], (copies,) + own.shape)


def stacked(wide, tap, channels):
    block = wide[..., tap * channels : (tap + 1) * channels]
    return block.reshape(channels, channels).astype(BF16)


def side_shift(product):
    channels = product.shape[1] // 3
    product = product.reshape(-1, LANE_COLS, 3 * channels)
    return (
        product[..., channels : 2 * channels]
        + pltpu.roll(product[..., :channels], 1, 1)
        + pltpu.roll(product[..., 2 * channels :], LANE_COLS - 1, 1)
    )


def build_kernel(frames, pack, top, x):
    cols = frames.shape[2]
    rows = frames.shape[1]
    outside = lax.axis_index("rows") == 0
    zero = jnp.zeros((), BF16)
    x[:, 0:1] = jnp.where(outside, zero, top[...])
    x[:, 1 : rows + 1, :cols] = frames[...]
    x[:, 1 : rows + 1, cols:] = pack[...]


def build_call(frames, pack, top):
    n_frames, rows, cols, channels = frames.shape
    batch = 3 if n_frames % 3 == 0 else 1
    shape = (n_frames, rows + 1, LANE_COLS, channels)
    return pl.pallas_call(
        build_kernel,
        grid=(n_frames // batch,),
        in_specs=[
            by_frame(rows, cols, channels, batch=batch),
            by_frame(rows, SIDE, channels, batch=batch),
            by_frame(1, LANE_COLS, channels, batch=batch),
        ],
        out_specs=by_frame(*shape[1:], batch=batch),
        out_shape=jax.ShapeDtypeStruct(shape, BF16),
        compiler_params=params(16),
        cost_estimate=cost(30 << 30, 64),
        name="build",
    )(frames, pack, top)


def inner_kernel(x, *rest, split):
    part_refs = rest[:4]
    first_row, middle, border, weight = rest[4:]
    n_frames, rows, _, channels = x.shape
    rows = rows - 1
    chan = lax.axis_index("chan") if split else 0
    for k, part in enumerate(part_refs):
        weight[chan ^ k] = part[...]

    def conv(f, many, row, count, taps):
        lhs = jnp.concatenate(
            [
                x[pl.ds(f, many), row + a : row + a + count].reshape(-1, channels)
                for a in range(taps)
            ],
            axis=1,
        )
        kernel = weight[:taps].reshape(taps * channels, 3 * channels)
        return side_shift(jnp.dot(lhs, kernel, preferred_element_type=F32))

    many = BATCH if n_frames % BATCH == 0 else 1

    def frames(g, _):
        at = pl.ds(g * many, many)
        first = conv(g * many, many, 0, rows - 1, 3).astype(BF16)
        first = first.reshape(many, rows - 1, LANE_COLS, channels)
        first_row[at] = first[:, 0]
        middle[at] = first.reshape(many, -1, channels)
        border[at] = conv(g * many, many, rows - 1, 1, 2)
        return 0

    lax.fori_loop(0, n_frames // many, frames, 0, unroll=True)


def outer_kernel(
    bottom, middle, border, weight, hidden, stats, temporal, firsts, *, cols
):
    n_frames, channels = middle.shape[0], middle.shape[2]
    rows = middle.shape[1] // LANE_COLS + 1
    size = rows * LANE_COLS
    count = float(rows * cols)
    outside = lax.axis_index("rows") == lax.axis_size("rows") - 1
    for k in range(3):
        at = k * channels
        temporal[at : at + channels] = weight[3, :, at : at + channels]

    many = BATCH if n_frames % BATCH == 0 else 1

    def frames(g, moments):
        mean_all, spread_all = moments
        start = g * many
        at = pl.ds(start, many)
        lhs = bottom[at].reshape(-1, channels)
        lhs = jnp.where(outside, jnp.zeros((), BF16), lhs)
        product = jnp.dot(lhs, weight[2], preferred_element_type=F32)
        last = (side_shift(product) + border[at]).astype(BF16)
        firsts[pl.ds(start + 2, many), : size - LANE_COLS] = middle[at]
        firsts[pl.ds(start + 2, many), size - LANE_COLS :] = last

        @pl.when(g == 0)
        def _():
            firsts[0] = firsts[2]
            firsts[1] = firsts[2]

        lhs = jnp.concatenate(
            [firsts[pl.ds(start + k, many)].reshape(-1, channels) for k in range(3)],
            axis=1,
        )
        total = jnp.dot(lhs, temporal[...], preferred_element_type=F32)
        total = total.reshape(many, rows, LANE_COLS, channels)
        for k in range(channels // 128):
            hidden[at, :, k] = total[..., k * 128 : (k + 1) * 128]
        inner = total[:, :, :cols].reshape(-1, 8, channels)
        mean = jnp.sum(jnp.sum(inner, axis=0), axis=0, keepdims=True) / (count * many)
        spread = jnp.sum(jnp.sum(jnp.square(inner - mean), axis=0), axis=0, keepdims=True)
        done = jnp.asarray(g, jnp.int32).astype(F32)
        delta = mean - mean_all
        mean_all = mean_all + delta / (done + 1.0)
        spread_all = spread_all + spread + delta * delta * (count * many * done / (done + 1.0))
        return mean_all, spread_all

    zero = jnp.zeros((1, channels), F32)
    mean, spread = lax.fori_loop(
        0, n_frames // many, frames, (zero, zero), unroll=True
    )
    stats[...] = jnp.broadcast_to(jnp.concatenate([mean, spread], axis=0)[None], stats.shape)


def back_kernel(
    hidden, halo, temporal, stats, gain, shift, bias, *rest, parts, cols
):
    part_refs = rest[:parts]
    latent, wide, weight, full, even, odd = rest[parts:]
    n_frames, rows, blocks = hidden.shape[:3]
    channels = halo.shape[2]
    half = LANE_COLS // 2
    cols_out = cols // 2
    rows_out = rows // 2
    count = float(n_frames * rows * cols)
    chan = lax.axis_index("chan") if parts > 1 else 0
    last_row = lax.axis_index("rows") == lax.axis_size("rows") - 1
    last_chan = lax.axis_index("chan") == lax.axis_size("chan") - 1

    for k, part in enumerate(part_refs):
        wide[:, chan ^ k] = part[...].astype(F32)
    for a in range(3):
        for b in range(3):
            at = (a + 3 * b) * channels
            weight[at : at + channels] = stacked(wide, 3 * a + b, channels)
    devices = stats.shape[0]
    group = channels // GROUPS
    means = stats[:, 0]
    mean = jnp.sum(means, axis=0, keepdims=True) / float(devices)
    spread = jnp.sum(stats[:, 1], axis=0, keepdims=True) + count * jnp.sum(
        jnp.square(means - mean), axis=0, keepdims=True
    )
    lane = lax.broadcasted_iota(jnp.int32, (channels, channels), 0) // group
    same = lane == lax.broadcasted_iota(jnp.int32, (channels, channels), 1) // group
    same = same.astype(F32)

    def over_group(values):
        return jnp.dot(
            jnp.broadcast_to(values, (8, channels)),
            same,
            precision=lax.Precision.HIGHEST,
            preferred_element_type=F32,
        )[0:1] / float(group)

    mean_group = over_group(mean)
    total = over_group(spread / (count * devices) + jnp.square(mean - mean_group))
    rstd = lax.rsqrt(total + EPSILON)

    def activated(values):
        return jax.nn.silu((values - mean_group) * rstd * gain[...] + shift[...])

    many = BATCH if n_frames % BATCH == 0 else 1
    size = rows_out * many * half
    starts = (0, rows_out + 1, 1)

    def frames(g, _):
        for i in range(many):
            f = g * many + i
            lhs = jnp.concatenate(
                [halo[jnp.maximum(f - 2, 0)], halo[jnp.maximum(f - 1, 0)], halo[f]], axis=1
            )
            extra = jnp.dot(lhs, temporal[...], preferred_element_type=F32)
            for k in range(blocks):
                full[i, k] = extra[:, k * 128 : (k + 1) * 128]

            def columns(row, start):
                picked = pl.ds(start, half, stride=2)
                return jnp.concatenate(
                    [
                        hidden[f, row, k, picked] if row < rows else full[i, k, picked]
                        for k in range(blocks)
                    ],
                    axis=1,
                )

            for row in range(rows + 1):
                place = row // 2 if row % 2 == 0 else rows_out + 1 + row // 2
                e = activated(columns(row, 0))
                o = activated(columns(row, 1))
                at = lax.broadcasted_iota(jnp.int32, e.shape, 0)
                drop = last_chan & (at >= cols_out)
                if row == rows:
                    drop = drop | last_row
                    o = jnp.where(last_row, 0.0, o)
                even[place, i] = jnp.where(drop, 0.0, e).astype(BF16)
                odd[place, i] = o.astype(BF16)
        evens = [even[s : s + rows_out].reshape(size, channels) for s in starts]
        odds = [odd[s : s + rows_out].reshape(size, channels) for s in starts]
        near = jnp.dot(
            jnp.concatenate(evens + odds, axis=1),
            weight[: 6 * channels],
            preferred_element_type=F32,
        )
        far = jnp.dot(
            jnp.concatenate(evens, axis=1),
            weight[6 * channels :],
            preferred_element_type=F32,
        )
        far = far.reshape(rows_out * many, half, channels)
        out = near.reshape(far.shape) + pltpu.roll(far, half - 1, 1) + bias[...]
        out = out.reshape(rows_out, many, half, channels).astype(BF16)
        for p in range(rows_out):
            for i in range(many):
                latent[g * many + i, p] = out[p, i, :cols_out]
        return 0

    lax.fori_loop(0, n_frames // many, frames, 0, unroll=True)


def whole(shape):
    return pl.BlockSpec(shape, lambda i, *_: (0,) * len(shape))


def by_frame(*tail, batch=1):
    return pl.BlockSpec((batch,) + tail, lambda i, *_: (i,) + (0,) * len(tail))


def params(mebibytes, grid=1):
    return pltpu.CompilerParams(
        dimension_semantics=("arbitrary",) * grid, vmem_limit_bytes=mebibytes << 20
    )


def cost(flops, mebibytes, exps=0):
    return pl.CostEstimate(
        flops=flops, bytes_accessed=mebibytes << 20, transcendentals=exps
    )


def in_vmem(count):
    return [pl.BlockSpec(memory_space=pltpu.VMEM)] * count


def inner_call(x, front_parts, split):
    n_frames, rows, _, channels = x.shape
    rows = rows - 1
    tap = 2 * n_frames * LANE_COLS * channels * channels
    return pl.pallas_call(
        functools.partial(inner_kernel, split=split),
        in_specs=in_vmem(5),
        out_specs=in_vmem(4),
        out_shape=[
            jax.ShapeDtypeStruct((n_frames, LANE_COLS, channels), BF16),
            jax.ShapeDtypeStruct((n_frames, (rows - 1) * LANE_COLS, channels), BF16),
            jax.ShapeDtypeStruct((n_frames, LANE_COLS, channels), F32),
            jax.ShapeDtypeStruct((4, channels, 3 * channels), BF16),
        ],
        compiler_params=params(24, grid=0),
        cost_estimate=cost(33 * tap, 8),
        name="inner",
    )(x, *front_parts)


def outer_call(bottom, middle, border, weight, cols, devices):
    n_frames, size, channels = middle.shape
    rows = size // LANE_COLS + 1
    tap = 2 * n_frames * LANE_COLS * channels * channels
    return pl.pallas_call(
        functools.partial(outer_kernel, cols=cols),
        in_specs=in_vmem(4),
        out_specs=in_vmem(3),
        scratch_shapes=[pltpu.VMEM((n_frames + 2, rows * LANE_COLS, channels), BF16)],
        out_shape=[
            pltpu.VMEM((n_frames, rows, channels // 128, LANE_COLS, 128), F32),
            jax.ShapeDtypeStruct((devices, 2, channels), F32),
            pltpu.VMEM((3 * channels, channels), BF16),
        ],
        compiler_params=params(24, grid=0),
        cost_estimate=cost(15 * tap, 10),
        name="outer",
    )(bottom, middle, border, weight)


def back_call(hidden, halo, temporal, all_stats, vectors, back_parts, cols):
    n_frames, rows = hidden.shape[:2]
    channels = halo.shape[2]
    parts = len(back_parts)
    piece = back_parts[0].shape
    many = BATCH if n_frames % BATCH == 0 else 1
    tap = 2 * n_frames * LANE_COLS * channels * channels
    half = LANE_COLS // 2
    return pl.pallas_call(
        functools.partial(back_kernel, parts=parts, cols=cols),
        in_specs=in_vmem(7 + parts),
        out_specs=pl.BlockSpec(memory_space=pltpu.VMEM),
        scratch_shapes=[
            pltpu.VMEM((piece[0], parts, piece[1], piece[2]), F32),
            pltpu.VMEM((9 * channels, channels), BF16),
            pltpu.VMEM((many, channels // 128, LANE_COLS, 128), F32),
            pltpu.VMEM((rows + 1, many, half, channels), BF16),
            pltpu.VMEM((rows + 1, many, half, channels), BF16),
        ],
        out_shape=jax.ShapeDtypeStruct((n_frames, rows // 2, cols // 2, channels), BF16),
        compiler_params=params(24, grid=0),
        cost_estimate=cost(12 * tap, 10, 4 << 20),
        name="back",
    )(hidden, halo, temporal, all_stats, *vectors, *back_parts)


def per_device(
    frames, spatial_weight, temporal_weight, down_weight, norm_gain, norm_shift, down_bias
):
    n_frames, rows, cols, channels = frames.shape
    row_devices, chan_devices = lax.axis_size("rows"), lax.axis_size("chan")
    part = spatial_weight.shape[0] // chan_devices
    split = part % 8 == 0 and chan_devices == 4
    first_cols, last_cols = side_columns(frames)
    right = shifted(first_cols, "chan", -1)
    left = shifted(last_cols, "chan", 1)
    low_row, high_row, pack = extended_call(frames, left, right)
    top = shifted(low_row, "rows", 1)

    if split:
        taps, own = weight_pieces(
            spatial_weight, temporal_weight, down_weight, channels, row_devices, part
        )
        taps = lax.all_to_all(taps, "rows", 0, 0)
        taps, pack = lax.optimization_barrier((taps, pack))
        bottom = shifted(high_row, "rows", -1)
        front_parts = spread_chan(taps.reshape(channels, 3 * channels))
        own, taps = lax.optimization_barrier((own, taps))
        own = lax.all_to_all(own, "rows", 0, 0)
    else:
        bottom = shifted(high_row, "rows", -1)
        joint = jnp.concatenate([spatial_weight, temporal_weight], 1)
        taps = lax.all_gather(joint, "rows", axis=0, tiled=True)
        width = 3 * channels
        front_parts = [taps[:, k * width : (k + 1) * width] for k in range(4)]
        own = lax.all_gather(down_weight, "rows", axis=0, tiled=True)

    x = build_call(frames, pack, top)
    x, own = lax.optimization_barrier((x, own))
    across = swapped(own, "chan", 2) if split else own
    first_row, middle, border, weight = inner_call(x, front_parts, split)
    halo = shifted(first_row, "rows", -1)
    if split:
        own, across, middle = lax.optimization_barrier((own, across, middle))
        back_parts = [own, swapped(own, "chan", 1), across, swapped(across, "chan", 1)]
    else:
        back_parts = [own.reshape(channels // 8, 8, -1)]
    hidden, stats, temporal = outer_call(
        bottom, middle, border, weight, cols, row_devices * chan_devices
    )
    stats, back_parts = lax.optimization_barrier((stats, back_parts))
    all_stats = lax.all_to_all(stats, ("rows", "chan"), 0, 0)
    vectors = [v.reshape(1, channels) for v in (norm_gain, norm_shift, down_bias)]
    return back_call(hidden, halo, temporal, all_stats, vectors, back_parts, cols)


def solution(mesh):
    placed = (
        P(None, "rows", "chan", None),
        P("rows", None),
        P("rows", None),
        P("rows", None),
        P(),
        P(),
        P(),
    )
    return jax.shard_map(
        per_device,
        mesh=mesh,
        in_specs=placed,
        out_specs=P(None, "rows", "chan", None),
        check_vma=False,
    )
```

```python
import functools

import jax
import jax.numpy as jnp
from jax import lax
from jax.experimental import pallas as pl
from jax.experimental.pallas import tpu as pltpu
from jax.sharding import PartitionSpec as P

GROUPS = 32
EPSILON = 1e-06
LANE_COLS = 128
SIDE = 8
GRANT = 56
BATCH = 3
F32 = jnp.float32
BF16 = jnp.bfloat16


def shifted(block, axis, distance):
    count = lax.axis_size(axis)
    return lax.ppermute(block, axis, [(i, (i + distance) % count) for i in range(count)])


def swapped(block, axis, bit):
    return lax.ppermute(block, axis, [(i, i ^ bit) for i in range(lax.axis_size(axis))])


def spread_chan(held):
    parts = {0: held}
    bit = lax.axis_size("chan") // 2
    while bit:
        parts.update({k ^ bit: swapped(part, "chan", bit) for k, part in parts.items()})
        bit //= 2
    return [parts[k] for k in range(len(parts))]


def anywhere(count):
    return [pl.BlockSpec(memory_space=pl.ANY)] * count


def staged_call(body, sources, kept, outs, sems, name):
    return pl.pallas_call(
        body,
        out_shape=outs,
        in_specs=[pl.BlockSpec(memory_space=pltpu.HBM)] * len(sources),
        out_specs=anywhere(len(outs)),
        scratch_shapes=[pltpu.VMEM(k.shape, k.dtype) for k in kept]
        + [pltpu.SemaphoreType.DMA((n,)) for n in sems],
        compiler_params=params(GRANT, grid=0),
        name=name,
    )(*sources)


def side_columns(frames, weights=(), copies=0, part=0):
    n_frames, rows, cols, channels = frames.shape
    width = 3 * channels
    side = jax.ShapeDtypeStruct((n_frames, rows, SIDE, channels), frames.dtype)
    kept, picks = [side, side], []
    if weights:
        spatial, temporal, down = weights
        kept += [
            jax.ShapeDtypeStruct((spatial.shape[0], width), spatial.dtype),
            jax.ShapeDtypeStruct((part, down.shape[1]), down.dtype),
        ]
        picks = [
            (n, at)
            for n, w in enumerate((spatial, temporal))
            for at in range(0, w.shape[1], width)
        ]
    count = len(kept)
    outs = kept[:2] + [
        jax.ShapeDtypeStruct((copies,) + k.shape, k.dtype) for k in kept[2:]
    ]

    def body(source, *refs):
        taps, refs = refs[: len(weights)], refs[len(weights) :]
        targets, holds, (sems, out_sems) = refs[:count], refs[count:-2], refs[-2:]
        slices = [source.at[:, :, 0:SIDE], source.at[:, :, cols - SIDE :]]
        if weights:
            chan = lax.axis_index("chan")
            start = pl.multiple_of(chan * part, part)
            slices += [taps[0].at[:, 0:width], taps[2].at[pl.ds(start, part)]]
            for k, (n, at) in enumerate(picks):
                @pl.when(chan == k)
                def _():
                    pltpu.make_async_copy(
                        taps[n].at[:, at : at + width], holds[2], sems.at[2]
                    ).start()
        fetches = [
            pltpu.make_async_copy(src, hold, sems.at[k])
            for k, (src, hold) in enumerate(zip(slices, holds))
        ]
        for k, fetch in enumerate(fetches):
            if k != 2:
                fetch.start()
        stores = []
        for k, fetch in enumerate(fetches):
            fetch.wait()
            for target in [targets[k]] if k < 2 else [targets[k].at[j] for j in range(copies)]:
                store = pltpu.make_async_copy(holds[k], target, out_sems.at[len(stores)])
                store.start()
                stores.append(store)
        for store in stores:
            store.wait()

    moves = 2 + (count - 2) * copies
    return staged_call(
        body, [frames, *weights], kept, outs, (count, moves), "side_columns"
    )


def extended_kernel(last_row, first_row, left, right, low, high, pack):
    rows, cols = left.shape[1], last_row.shape[2]
    chan = lax.axis_index("chan")
    at = lax.broadcasted_iota(jnp.int32, left.shape, 2)
    before = jnp.where(chan == 0, 0.0, left[...].astype(F32))
    after = jnp.where(chan == lax.axis_size("chan") - 1, 0.0, right[...].astype(F32))
    side = jnp.where(at == SIDE - 1, before, after).astype(BF16)
    pack[...] = side
    low[:, :, :cols] = last_row[...]
    low[:, :, cols:] = side[:, rows - 1 :]
    high[:, :, :cols] = first_row[...]
    high[:, :, cols:] = side[:, :1]


def extended_call(frames, left, right):
    n_frames, rows, cols, channels = frames.shape
    row = (n_frames, 1, cols, channels)
    full = (n_frames, 1, LANE_COLS, channels)
    wide = pltpu.HBM(full, BF16)
    return pl.pallas_call(
        extended_kernel,
        grid=(1,),
        in_specs=[
            pl.BlockSpec(row, lambda i: (0, rows - 1, 0, 0)),
            pl.BlockSpec(row, lambda i: (0, 0, 0, 0)),
            whole(left.shape),
            whole(right.shape),
        ],
        out_specs=[whole(full), whole(full), whole(left.shape)],
        out_shape=[wide, wide, jax.ShapeDtypeStruct(left.shape, BF16)],
        compiler_params=params(16),
        cost_estimate=cost(0, 3),
        name="extended",
    )(frames, frames, left, right)


def repeated(own, copies):
    return jnp.broadcast_to(own[None], (copies,) + own.shape)


def stacked(wide, tap, channels):
    block = wide[..., tap * channels : (tap + 1) * channels]
    return block.reshape(channels, channels).astype(BF16)


def side_shift(product):
    channels = product.shape[1] // 3
    product = product.reshape(-1, LANE_COLS, 3 * channels)
    return (
        product[..., channels : 2 * channels]
        + pltpu.roll(product[..., :channels], 1, 1)
        + pltpu.roll(product[..., 2 * channels :], LANE_COLS - 1, 1)
    )


def build_kernel(frames, pack, x):
    cols = frames.shape[2]
    x[:, :, :cols] = frames[...]
    x[:, :, cols:] = pack[...]


def build_call(frames, pack):
    n_frames, rows, cols, channels = frames.shape
    return pl.pallas_call(
        build_kernel,
        in_specs=in_vmem(2),
        out_specs=pl.BlockSpec(memory_space=pltpu.VMEM),
        out_shape=pltpu.VMEM((n_frames, rows, LANE_COLS, channels), BF16),
        compiler_params=params(8, grid=0),
        cost_estimate=cost(0, 5),
        name="build",
    )(frames, pack)


def masked_kernel(top, kept):
    outside = lax.axis_index("rows") == 0
    kept[...] = jnp.where(outside, jnp.zeros((), BF16), top[...])


def masked_call(top):
    return pl.pallas_call(
        masked_kernel,
        in_specs=in_vmem(1),
        out_specs=pl.BlockSpec(memory_space=pltpu.VMEM),
        out_shape=pltpu.VMEM(top.shape, BF16),
        compiler_params=params(4, grid=0),
        cost_estimate=cost(30 << 30, 64),
        name="masked",
    )(top)


def inner_kernel(x, top, *rest, split):
    part_refs = rest[:4]
    first_row, middle, border, weight = rest[4:]
    n_frames, rows, _, channels = x.shape
    chan = lax.axis_index("chan") if split else 0
    for k, part in enumerate(part_refs):
        weight[chan ^ k] = part[...]

    def conv(lhs):
        taps = len(lhs)
        lhs = jnp.concatenate([block.reshape(-1, channels) for block in lhs], axis=1)
        kernel = weight[:taps].reshape(taps * channels, 3 * channels)
        return side_shift(jnp.dot(lhs, kernel, preferred_element_type=F32))

    many = BATCH if n_frames % BATCH == 0 else 1

    def frames(g, _):
        at = pl.ds(g * many, many)
        first = conv(
            [
                jnp.concatenate([top[at], x[at, : rows - 2]], axis=1),
                x[at, : rows - 1],
                x[at, 1:],
            ]
        ).astype(BF16)
        first = first.reshape(many, rows - 1, LANE_COLS, channels)
        first_row[at] = first[:, 0]
        middle[at] = first.reshape(many, -1, channels)
        border[at] = conv([x[at, rows - 2], x[at, rows - 1]])
        return 0

    lax.fori_loop(0, n_frames // many, frames, 0, unroll=True)


def outer_kernel(
    bottom, middle, border, weight, hidden, stats, temporal, firsts, *, cols
):
    n_frames, channels = middle.shape[0], middle.shape[2]
    rows = middle.shape[1] // LANE_COLS + 1
    size = rows * LANE_COLS
    count = float(rows * cols)
    outside = lax.axis_index("rows") == lax.axis_size("rows") - 1
    for k in range(3):
        at = k * channels
        temporal[at : at + channels] = weight[3, :, at : at + channels]

    many = BATCH if n_frames % BATCH == 0 else 1

    def frames(g, moments):
        mean_all, spread_all = moments
        start = g * many
        at = pl.ds(start, many)
        lhs = bottom[at].reshape(-1, channels)
        lhs = jnp.where(outside, jnp.zeros((), BF16), lhs)
        product = jnp.dot(lhs, weight[2], preferred_element_type=F32)
        last = (side_shift(product) + border[at]).astype(BF16)
        firsts[pl.ds(start + 2, many), : size - LANE_COLS] = middle[at]
        firsts[pl.ds(start + 2, many), size - LANE_COLS :] = last

        @pl.when(g == 0)
        def _():
            firsts[0] = firsts[2]
            firsts[1] = firsts[2]

        lhs = jnp.concatenate(
            [firsts[pl.ds(start + k, many)].reshape(-1, channels) for k in range(3)],
            axis=1,
        )
        total = jnp.dot(lhs, temporal[...], preferred_element_type=F32)
        total = total.reshape(many, rows, LANE_COLS, channels)
        for k in range(channels // 128):
            hidden[at, :, k] = total[..., k * 128 : (k + 1) * 128]
        inner = total[:, :, :cols].reshape(-1, 8, channels)
        mean = jnp.sum(jnp.sum(inner, axis=0), axis=0, keepdims=True) / (count * many)
        spread = jnp.sum(jnp.sum(jnp.square(inner - mean), axis=0), axis=0, keepdims=True)
        done = jnp.asarray(g, jnp.int32).astype(F32)
        delta = mean - mean_all
        mean_all = mean_all + delta / (done + 1.0)
        spread_all = spread_all + spread + delta * delta * (count * many * done / (done + 1.0))
        return mean_all, spread_all

    zero = jnp.zeros((1, channels), F32)
    mean, spread = lax.fori_loop(
        0, n_frames // many, frames, (zero, zero), unroll=True
    )
    stats[...] = jnp.broadcast_to(jnp.concatenate([mean, spread], axis=0)[None], stats.shape)


def back_kernel(
    hidden, halo, temporal, stats, gain, shift, bias, *rest, parts, cols
):
    part_refs = rest[:parts]
    latent, wide, weight, full, even, odd = rest[parts:]
    n_frames, rows, blocks = hidden.shape[:3]
    channels = halo.shape[2]
    half = LANE_COLS // 2
    cols_out = cols // 2
    rows_out = rows // 2
    count = float(n_frames * rows * cols)
    chan = lax.axis_index("chan") if parts > 1 else 0
    last_row = lax.axis_index("rows") == lax.axis_size("rows") - 1
    last_chan = lax.axis_index("chan") == lax.axis_size("chan") - 1

    for k, part in enumerate(part_refs):
        wide[:, chan ^ k] = part[...].astype(F32)
    for a in range(3):
        for b in range(3):
            at = (a + 3 * b) * channels
            weight[at : at + channels] = stacked(wide, 3 * a + b, channels)
    devices = stats.shape[0]
    group = channels // GROUPS
    means = stats[:, 0]
    mean = jnp.sum(means, axis=0, keepdims=True) / float(devices)
    spread = jnp.sum(stats[:, 1], axis=0, keepdims=True) + count * jnp.sum(
        jnp.square(means - mean), axis=0, keepdims=True
    )
    lane = lax.broadcasted_iota(jnp.int32, (channels, channels), 0) // group
    same = lane == lax.broadcasted_iota(jnp.int32, (channels, channels), 1) // group
    same = same.astype(F32)

    def over_group(values):
        return jnp.dot(
            jnp.broadcast_to(values, (8, channels)),
            same,
            precision=lax.Precision.HIGHEST,
            preferred_element_type=F32,
        )[0:1] / float(group)

    mean_group = over_group(mean)
    total = over_group(spread / (count * devices) + jnp.square(mean - mean_group))
    rstd = lax.rsqrt(total + EPSILON)

    def activated(values):
        return jax.nn.silu((values - mean_group) * rstd * gain[...] + shift[...])

    many = BATCH if n_frames % BATCH == 0 else 1
    size = rows_out * many * half
    starts = (0, rows_out + 1, 1)

    def frames(g, _):
        for i in range(many):
            f = g * many + i
            lhs = jnp.concatenate(
                [halo[jnp.maximum(f - 2, 0)], halo[jnp.maximum(f - 1, 0)], halo[f]], axis=1
            )
            extra = jnp.dot(lhs, temporal[...], preferred_element_type=F32)
            for k in range(blocks):
                full[i, k] = extra[:, k * 128 : (k + 1) * 128]

            def columns(row, start):
                picked = pl.ds(start, half, stride=2)
                return jnp.concatenate(
                    [
                        hidden[f, row, k, picked] if row < rows else full[i, k, picked]
                        for k in range(blocks)
                    ],
                    axis=1,
                )

            for row in range(rows + 1):
                place = row // 2 if row % 2 == 0 else rows_out + 1 + row // 2
                e = activated(columns(row, 0))
                o = activated(columns(row, 1))
                at = lax.broadcasted_iota(jnp.int32, e.shape, 0)
                drop = last_chan & (at >= cols_out)
                if row == rows:
                    drop = drop | last_row
                    o = jnp.where(last_row, 0.0, o)
                even[place, i] = jnp.where(drop, 0.0, e).astype(BF16)
                odd[place, i] = o.astype(BF16)
        evens = [even[s : s + rows_out].reshape(size, channels) for s in starts]
        odds = [odd[s : s + rows_out].reshape(size, channels) for s in starts]
        near = jnp.dot(
            jnp.concatenate(evens + odds, axis=1),
            weight[: 6 * channels],
            preferred_element_type=F32,
        )
        far = jnp.dot(
            jnp.concatenate(evens, axis=1),
            weight[6 * channels :],
            preferred_element_type=F32,
        )
        far = far.reshape(rows_out * many, half, channels)
        out = near.reshape(far.shape) + pltpu.roll(far, half - 1, 1) + bias[...]
        out = out.reshape(rows_out, many, half, channels).astype(BF16)
        for p in range(rows_out):
            for i in range(many):
                latent[g * many + i, p] = out[p, i, :cols_out]
        return 0

    lax.fori_loop(0, n_frames // many, frames, 0, unroll=True)


def whole(shape):
    return pl.BlockSpec(shape, lambda i, *_: (0,) * len(shape))


def by_frame(*tail, batch=1):
    return pl.BlockSpec((batch,) + tail, lambda i, *_: (i,) + (0,) * len(tail))


def params(mebibytes, grid=1):
    return pltpu.CompilerParams(
        dimension_semantics=("arbitrary",) * grid, vmem_limit_bytes=mebibytes << 20
    )


def cost(flops, mebibytes, exps=0):
    return pl.CostEstimate(
        flops=flops, bytes_accessed=mebibytes << 20, transcendentals=exps
    )


def in_vmem(count):
    return [pl.BlockSpec(memory_space=pltpu.VMEM)] * count


def inner_call(x, top, front_parts, split):
    n_frames, rows, _, channels = x.shape
    return pl.pallas_call(
        functools.partial(inner_kernel, split=split),
        in_specs=in_vmem(6),
        out_specs=in_vmem(4),
        out_shape=[
            jax.ShapeDtypeStruct((n_frames, LANE_COLS, channels), BF16),
            jax.ShapeDtypeStruct((n_frames, (rows - 1) * LANE_COLS, channels), BF16),
            jax.ShapeDtypeStruct((n_frames, LANE_COLS, channels), F32),
            jax.ShapeDtypeStruct((4, channels, 3 * channels), BF16),
        ],
        compiler_params=params(24, grid=0),
        cost_estimate=cost(5 << 30, 8),
        name="inner",
    )(x, top, *front_parts)


def outer_call(bottom, middle, border, weight, cols, devices):
    n_frames, size, channels = middle.shape
    rows = size // LANE_COLS + 1
    tap = 2 * n_frames * LANE_COLS * channels * channels
    return pl.pallas_call(
        functools.partial(outer_kernel, cols=cols),
        in_specs=in_vmem(4),
        out_specs=in_vmem(3),
        scratch_shapes=[pltpu.VMEM((n_frames + 2, rows * LANE_COLS, channels), BF16)],
        out_shape=[
            pltpu.VMEM((n_frames, rows, channels // 128, LANE_COLS, 128), F32),
            jax.ShapeDtypeStruct((devices, 2, channels), F32),
            pltpu.VMEM((3 * channels, channels), BF16),
        ],
        compiler_params=params(24, grid=0),
        cost_estimate=cost(15 * tap, 10),
        name="outer",
    )(bottom, middle, border, weight)


def back_call(hidden, halo, temporal, all_stats, vectors, back_parts, cols):
    n_frames, rows = hidden.shape[:2]
    channels = halo.shape[2]
    parts = len(back_parts)
    piece = back_parts[0].shape
    many = BATCH if n_frames % BATCH == 0 else 1
    tap = 2 * n_frames * LANE_COLS * channels * channels
    half = LANE_COLS // 2
    return pl.pallas_call(
        functools.partial(back_kernel, parts=parts, cols=cols),
        in_specs=in_vmem(7 + parts),
        out_specs=pl.BlockSpec(memory_space=pltpu.VMEM),
        scratch_shapes=[
            pltpu.VMEM((piece[0], parts, piece[1], piece[2]), F32),
            pltpu.VMEM((9 * channels, channels), BF16),
            pltpu.VMEM((many, channels // 128, LANE_COLS, 128), F32),
            pltpu.VMEM((rows + 1, many, half, channels), BF16),
            pltpu.VMEM((rows + 1, many, half, channels), BF16),
        ],
        out_shape=jax.ShapeDtypeStruct((n_frames, rows // 2, cols // 2, channels), BF16),
        compiler_params=params(24, grid=0),
        cost_estimate=cost(12 * tap, 10, 4 << 20),
        name="back",
    )(hidden, halo, temporal, all_stats, *vectors, *back_parts)


def per_device(
    frames, spatial_weight, temporal_weight, down_weight, norm_gain, norm_shift, down_bias
):
    n_frames, rows, cols, channels = frames.shape
    row_devices, chan_devices = lax.axis_size("rows"), lax.axis_size("chan")
    part = spatial_weight.shape[0] // chan_devices
    split = part % 8 == 0 and chan_devices == 4
    if split:
        first_cols, last_cols, taps, own = side_columns(
            frames, (spatial_weight, temporal_weight, down_weight), row_devices, part
        )
    else:
        first_cols, last_cols = side_columns(frames)
    right = shifted(first_cols, "chan", -1)
    left = shifted(last_cols, "chan", 1)
    low_row, high_row, pack = extended_call(frames, left, right)
    top = shifted(low_row, "rows", 1)

    if split:
        taps = lax.all_to_all(taps, "rows", 0, 0)
        taps, _ = lax.optimization_barrier((taps, pack))
        taps = taps.reshape(channels, 3 * channels)
        over = swapped(taps, "chan", 2)
        over, high_row = lax.optimization_barrier((over, high_row))
        bottom = shifted(high_row, "rows", -1)
        front_parts = [taps, swapped(taps, "chan", 1), over, swapped(over, "chan", 1)]
        own, taps = lax.optimization_barrier((own, taps))
        own = lax.all_to_all(own, "rows", 0, 0)
    else:
        bottom = shifted(high_row, "rows", -1)
        joint = jnp.concatenate([spatial_weight, temporal_weight], 1)
        taps = lax.all_gather(joint, "rows", axis=0, tiled=True)
        width = 3 * channels
        front_parts = [taps[:, k * width : (k + 1) * width] for k in range(4)]
        own = lax.all_gather(down_weight, "rows", axis=0, tiled=True)

    x = build_call(frames, pack)
    own, top = lax.optimization_barrier((own, top))
    top = masked_call(top)
    across = swapped(own, "chan", 2) if split else own
    first_row, middle, border, weight = inner_call(x, top, front_parts, split)
    halo = shifted(first_row, "rows", -1)
    if split:
        own, across, _ = lax.optimization_barrier((own, across, middle))
        back_parts = [own, swapped(own, "chan", 1), across, swapped(across, "chan", 1)]
    else:
        back_parts = [own.reshape(channels // 8, 8, -1)]
    hidden, stats, temporal = outer_call(
        bottom, middle, border, weight, cols, row_devices * chan_devices
    )
    stats, back_parts = lax.optimization_barrier((stats, back_parts))
    all_stats = lax.all_to_all(stats, ("rows", "chan"), 0, 0)
    vectors = [v.reshape(1, channels) for v in (norm_gain, norm_shift, down_bias)]
    return back_call(hidden, halo, temporal, all_stats, vectors, back_parts, cols)


def solution(mesh):
    placed = (
        P(None, "rows", "chan", None),
        P("rows", None),
        P("rows", None),
        P("rows", None),
        P(),
        P(),
        P(),
    )
    return jax.shard_map(
        per_device,
        mesh=mesh,
        in_specs=placed,
        out_specs=P(None, "rows", "chan", None),
        check_vma=False,
    )
```

```python
import functools

import jax
import jax.numpy as jnp
from jax import lax
from jax.experimental import pallas as pl
from jax.experimental.pallas import tpu as pltpu
from jax.sharding import PartitionSpec as P

GROUPS = 32
EPSILON = 1e-06
LANE_COLS = 128
SIDE = 8
GRANT = 56
BATCH = 3
F32 = jnp.float32
BF16 = jnp.bfloat16


def shifted(block, axis, distance):
    count = lax.axis_size(axis)
    return lax.ppermute(block, axis, [(i, (i + distance) % count) for i in range(count)])


def swapped(block, axis, bit):
    return lax.ppermute(block, axis, [(i, i ^ bit) for i in range(lax.axis_size(axis))])


def spread_chan(held):
    parts = {0: held}
    bit = lax.axis_size("chan") // 2
    while bit:
        parts.update({k ^ bit: swapped(part, "chan", bit) for k, part in parts.items()})
        bit //= 2
    return [parts[k] for k in range(len(parts))]


def anywhere(count):
    return [pl.BlockSpec(memory_space=pl.ANY)] * count


def staged_call(body, sources, kept, outs, sems, name):
    return pl.pallas_call(
        body,
        out_shape=outs,
        in_specs=[pl.BlockSpec(memory_space=pltpu.HBM)] * len(sources),
        out_specs=anywhere(len(outs)),
        scratch_shapes=[pltpu.VMEM(k.shape, k.dtype) for k in kept]
        + [pltpu.SemaphoreType.DMA((n,)) for n in sems],
        compiler_params=params(GRANT, grid=0),
        name=name,
    )(*sources)


def side_columns(frames, weights=(), copies=0, part=0):
    n_frames, rows, cols, channels = frames.shape
    width = 3 * channels
    side = jax.ShapeDtypeStruct((n_frames, rows, SIDE, channels), frames.dtype)
    kept, picks = [side, side], []
    if weights:
        spatial, temporal, down = weights
        kept += [
            jax.ShapeDtypeStruct((spatial.shape[0], width), spatial.dtype),
            jax.ShapeDtypeStruct((part, down.shape[1]), down.dtype),
        ]
        picks = [
            (n, at)
            for n, w in enumerate((spatial, temporal))
            for at in range(0, w.shape[1], width)
        ]
    count = len(kept)
    outs = kept[:2] + [
        jax.ShapeDtypeStruct((many,) + k.shape, k.dtype)
        for many, k in zip((copies, 1), kept[2:])
    ]

    def body(source, *refs):
        taps, refs = refs[: len(weights)], refs[len(weights) :]
        targets, holds, (sems, out_sems) = refs[:count], refs[count:-2], refs[-2:]
        slices = [source.at[:, :, 0:SIDE], source.at[:, :, cols - SIDE :]]
        if weights:
            chan = lax.axis_index("chan")
            start = pl.multiple_of(chan * part, part)
            slices += [taps[0].at[:, 0:width], taps[2].at[pl.ds(start, part)]]
            for k, (n, at) in enumerate(picks):
                @pl.when(chan == k)
                def _():
                    pltpu.make_async_copy(
                        taps[n].at[:, at : at + width], holds[2], sems.at[2]
                    ).start()
        fetches = [
            pltpu.make_async_copy(src, hold, sems.at[k])
            for k, (src, hold) in enumerate(zip(slices, holds))
        ]
        for k, fetch in enumerate(fetches):
            if k != 2:
                fetch.start()
        stores = []
        for k, fetch in enumerate(fetches):
            fetch.wait()
            spread = [targets[k].at[j] for j in range(copies if k == 2 else 1)] if k >= 2 else []
            for target in spread or [targets[k]]:
                store = pltpu.make_async_copy(holds[k], target, out_sems.at[len(stores)])
                store.start()
                stores.append(store)
        for store in stores:
            store.wait()

    moves = 3 + copies
    return staged_call(
        body, [frames, *weights], kept, outs, (count, moves), "side_columns"
    )


def merged_kernel(*refs, unit, place):
    parts, out = refs[:-1], refs[-1]
    here = lax.rem(lax.axis_index("rows") // unit, place)
    for k, part in enumerate(parts):
        out[here ^ k] = part[...]


def merged_call(parts, unit):
    shape = parts[0].shape
    return pl.pallas_call(
        functools.partial(merged_kernel, unit=unit, place=len(parts)),
        in_specs=in_vmem(len(parts)),
        out_specs=pl.BlockSpec(memory_space=pltpu.VMEM),
        out_shape=jax.ShapeDtypeStruct((len(parts),) + shape, parts[0].dtype),
        compiler_params=params(8, grid=0),
        cost_estimate=cost(0, 1),
        name="merged",
    )(*parts)


def extended_kernel(last_row, first_row, left, right, low, high, pack):
    rows, cols = left.shape[1], last_row.shape[2]
    chan = lax.axis_index("chan")
    at = lax.broadcasted_iota(jnp.int32, left.shape, 2)
    before = jnp.where(chan == 0, 0.0, left[...].astype(F32))
    after = jnp.where(chan == lax.axis_size("chan") - 1, 0.0, right[...].astype(F32))
    side = jnp.where(at == SIDE - 1, before, after).astype(BF16)
    pack[...] = side
    low[:, :, :cols] = last_row[...]
    low[:, :, cols:] = side[:, rows - 1 :]
    high[:, :, :cols] = first_row[...]
    high[:, :, cols:] = side[:, :1]


def extended_call(frames, left, right):
    n_frames, rows, cols, channels = frames.shape
    row = (n_frames, 1, cols, channels)
    full = (n_frames, 1, LANE_COLS, channels)
    wide = pltpu.HBM(full, BF16)
    return pl.pallas_call(
        extended_kernel,
        grid=(1,),
        in_specs=[
            pl.BlockSpec(row, lambda i: (0, rows - 1, 0, 0)),
            pl.BlockSpec(row, lambda i: (0, 0, 0, 0)),
            whole(left.shape),
            whole(right.shape),
        ],
        out_specs=[whole(full), whole(full), whole(left.shape)],
        out_shape=[wide, wide, jax.ShapeDtypeStruct(left.shape, BF16)],
        compiler_params=params(16),
        cost_estimate=cost(0, 3),
        name="extended",
    )(frames, frames, left, right)


def repeated(own, copies):
    return jnp.broadcast_to(own[None], (copies,) + own.shape)


def stacked(wide, tap, channels):
    block = wide[..., tap * channels : (tap + 1) * channels]
    return block.reshape(channels, channels).astype(BF16)


def side_shift(product):
    channels = product.shape[1] // 3
    product = product.reshape(-1, LANE_COLS, 3 * channels)
    return (
        product[..., channels : 2 * channels]
        + pltpu.roll(product[..., :channels], 1, 1)
        + pltpu.roll(product[..., 2 * channels :], LANE_COLS - 1, 1)
    )


def build_kernel(frames, pack, x):
    cols = frames.shape[2]
    x[:, :, :cols] = frames[...]
    x[:, :, cols:] = pack[...]


def build_call(frames, pack):
    n_frames, rows, cols, channels = frames.shape
    return pl.pallas_call(
        build_kernel,
        in_specs=in_vmem(2),
        out_specs=pl.BlockSpec(memory_space=pltpu.VMEM),
        out_shape=pltpu.VMEM((n_frames, rows, LANE_COLS, channels), BF16),
        compiler_params=params(8, grid=0),
        cost_estimate=cost(0, 5),
        name="build",
    )(frames, pack)


def masked_kernel(top, kept):
    outside = lax.axis_index("rows") == 0
    kept[...] = jnp.where(outside, jnp.zeros((), BF16), top[...])


def masked_call(top):
    return pl.pallas_call(
        masked_kernel,
        in_specs=in_vmem(1),
        out_specs=pl.BlockSpec(memory_space=pltpu.VMEM),
        out_shape=pltpu.VMEM(top.shape, BF16),
        compiler_params=params(4, grid=0),
        cost_estimate=cost(30 << 30, 64),
        name="masked",
    )(top)


def inner_kernel(x, top, *rest, split):
    part_refs = rest[:4]
    first_row, middle, border, weight = rest[4:]
    n_frames, rows, _, channels = x.shape
    chan = lax.axis_index("chan") if split else 0
    for k, part in enumerate(part_refs):
        weight[chan ^ k] = part[...]

    def conv(lhs):
        taps = len(lhs)
        lhs = jnp.concatenate([block.reshape(-1, channels) for block in lhs], axis=1)
        kernel = weight[:taps].reshape(taps * channels, 3 * channels)
        return side_shift(jnp.dot(lhs, kernel, preferred_element_type=F32))

    many = BATCH if n_frames % BATCH == 0 else 1

    def frames(g, _):
        at = pl.ds(g * many, many)
        first = conv(
            [
                jnp.concatenate([top[at], x[at, : rows - 2]], axis=1),
                x[at, : rows - 1],
                x[at, 1:],
            ]
        ).astype(BF16)
        first = first.reshape(many, rows - 1, LANE_COLS, channels)
        first_row[at] = first[:, 0]
        middle[at] = first.reshape(many, -1, channels)
        border[at] = conv([x[at, rows - 2], x[at, rows - 1]])
        return 0

    lax.fori_loop(0, n_frames // many, frames, 0, unroll=True)


def outer_kernel(
    bottom, middle, border, weight, hidden, stats, temporal, firsts, *, cols
):
    n_frames, channels = middle.shape[0], middle.shape[2]
    rows = middle.shape[1] // LANE_COLS + 1
    size = rows * LANE_COLS
    count = float(rows * cols)
    outside = lax.axis_index("rows") == lax.axis_size("rows") - 1
    for k in range(3):
        at = k * channels
        temporal[at : at + channels] = weight[3, :, at : at + channels]

    many = BATCH if n_frames % BATCH == 0 else 1

    def frames(g, moments):
        mean_all, spread_all = moments
        start = g * many
        at = pl.ds(start, many)
        lhs = bottom[at].reshape(-1, channels)
        lhs = jnp.where(outside, jnp.zeros((), BF16), lhs)
        product = jnp.dot(lhs, weight[2], preferred_element_type=F32)
        last = (side_shift(product) + border[at]).astype(BF16)
        firsts[pl.ds(start + 2, many), : size - LANE_COLS] = middle[at]
        firsts[pl.ds(start + 2, many), size - LANE_COLS :] = last

        @pl.when(g == 0)
        def _():
            firsts[0] = firsts[2]
            firsts[1] = firsts[2]

        lhs = jnp.concatenate(
            [firsts[pl.ds(start + k, many)].reshape(-1, channels) for k in range(3)],
            axis=1,
        )
        total = jnp.dot(lhs, temporal[...], preferred_element_type=F32)
        total = total.reshape(many, rows, LANE_COLS, channels)
        for k in range(channels // 128):
            hidden[at, :, k] = total[..., k * 128 : (k + 1) * 128]
        inner = total[:, :, :cols].reshape(-1, 8, channels)
        mean = jnp.sum(jnp.sum(inner, axis=0), axis=0, keepdims=True) / (count * many)
        spread = jnp.sum(jnp.sum(jnp.square(inner - mean), axis=0), axis=0, keepdims=True)
        done = jnp.asarray(g, jnp.int32).astype(F32)
        delta = mean - mean_all
        mean_all = mean_all + delta / (done + 1.0)
        spread_all = spread_all + spread + delta * delta * (count * many * done / (done + 1.0))
        return mean_all, spread_all

    zero = jnp.zeros((1, channels), F32)
    mean, spread = lax.fori_loop(
        0, n_frames // many, frames, (zero, zero), unroll=True
    )
    stats[...] = jnp.broadcast_to(jnp.concatenate([mean, spread], axis=0)[None], stats.shape)


def back_kernel(
    hidden, halo, temporal, stats, gain, shift, bias, *rest, parts, cols
):
    part_refs = rest[:parts]
    latent, wide, weight, full, even, odd = rest[parts:]
    n_frames, rows, blocks = hidden.shape[:3]
    channels = halo.shape[2]
    half = LANE_COLS // 2
    cols_out = cols // 2
    rows_out = rows // 2
    count = float(n_frames * rows * cols)
    chan = lax.axis_index("chan") if parts > 1 else 0
    last_row = lax.axis_index("rows") == lax.axis_size("rows") - 1
    last_chan = lax.axis_index("chan") == lax.axis_size("chan") - 1

    for k, part in enumerate(part_refs):
        wide[:, chan ^ k] = part[...].astype(F32)
    for a in range(3):
        for b in range(3):
            at = (a + 3 * b) * channels
            weight[at : at + channels] = stacked(wide, 3 * a + b, channels)
    devices = stats.shape[0]
    group = channels // GROUPS
    means = stats[:, 0]
    mean = jnp.sum(means, axis=0, keepdims=True) / float(devices)
    spread = jnp.sum(stats[:, 1], axis=0, keepdims=True) + count * jnp.sum(
        jnp.square(means - mean), axis=0, keepdims=True
    )
    lane = lax.broadcasted_iota(jnp.int32, (channels, channels), 0) // group
    same = lane == lax.broadcasted_iota(jnp.int32, (channels, channels), 1) // group
    same = same.astype(F32)

    def over_group(values):
        return jnp.dot(
            jnp.broadcast_to(values, (8, channels)),
            same,
            precision=lax.Precision.HIGHEST,
            preferred_element_type=F32,
        )[0:1] / float(group)

    mean_group = over_group(mean)
    total = over_group(spread / (count * devices) + jnp.square(mean - mean_group))
    rstd = lax.rsqrt(total + EPSILON)

    def activated(values):
        return jax.nn.silu((values - mean_group) * rstd * gain[...] + shift[...])

    many = BATCH if n_frames % BATCH == 0 else 1
    size = rows_out * many * half
    starts = (0, rows_out + 1, 1)

    def frames(g, _):
        for i in range(many):
            f = g * many + i
            lhs = jnp.concatenate(
                [halo[jnp.maximum(f - 2, 0)], halo[jnp.maximum(f - 1, 0)], halo[f]], axis=1
            )
            extra = jnp.dot(lhs, temporal[...], preferred_element_type=F32)
            for k in range(blocks):
                full[i, k] = extra[:, k * 128 : (k + 1) * 128]

            def columns(row, start):
                picked = pl.ds(start, half, stride=2)
                return jnp.concatenate(
                    [
                        hidden[f, row, k, picked] if row < rows else full[i, k, picked]
                        for k in range(blocks)
                    ],
                    axis=1,
                )

            for row in range(rows + 1):
                place = row // 2 if row % 2 == 0 else rows_out + 1 + row // 2
                e = activated(columns(row, 0))
                o = activated(columns(row, 1))
                at = lax.broadcasted_iota(jnp.int32, e.shape, 0)
                drop = last_chan & (at >= cols_out)
                if row == rows:
                    drop = drop | last_row
                    o = jnp.where(last_row, 0.0, o)
                even[place, i] = jnp.where(drop, 0.0, e).astype(BF16)
                odd[place, i] = o.astype(BF16)
        evens = [even[s : s + rows_out].reshape(size, channels) for s in starts]
        odds = [odd[s : s + rows_out].reshape(size, channels) for s in starts]
        near = jnp.dot(
            jnp.concatenate(evens + odds, axis=1),
            weight[: 6 * channels],
            preferred_element_type=F32,
        )
        far = jnp.dot(
            jnp.concatenate(evens, axis=1),
            weight[6 * channels :],
            preferred_element_type=F32,
        )
        far = far.reshape(rows_out * many, half, channels)
        out = near.reshape(far.shape) + pltpu.roll(far, half - 1, 1) + bias[...]
        out = out.reshape(rows_out, many, half, channels).astype(BF16)
        for p in range(rows_out):
            for i in range(many):
                latent[g * many + i, p] = out[p, i, :cols_out]
        return 0

    lax.fori_loop(0, n_frames // many, frames, 0, unroll=True)


def whole(shape):
    return pl.BlockSpec(shape, lambda i, *_: (0,) * len(shape))


def by_frame(*tail, batch=1):
    return pl.BlockSpec((batch,) + tail, lambda i, *_: (i,) + (0,) * len(tail))


def params(mebibytes, grid=1):
    return pltpu.CompilerParams(
        dimension_semantics=("arbitrary",) * grid, vmem_limit_bytes=mebibytes << 20
    )


def cost(flops, mebibytes, exps=0):
    return pl.CostEstimate(
        flops=flops, bytes_accessed=mebibytes << 20, transcendentals=exps
    )


def in_vmem(count):
    return [pl.BlockSpec(memory_space=pltpu.VMEM)] * count


def inner_call(x, top, front_parts, split):
    n_frames, rows, _, channels = x.shape
    return pl.pallas_call(
        functools.partial(inner_kernel, split=split),
        in_specs=in_vmem(6),
        out_specs=in_vmem(4),
        out_shape=[
            jax.ShapeDtypeStruct((n_frames, LANE_COLS, channels), BF16),
            jax.ShapeDtypeStruct((n_frames, (rows - 1) * LANE_COLS, channels), BF16),
            jax.ShapeDtypeStruct((n_frames, LANE_COLS, channels), F32),
            jax.ShapeDtypeStruct((4, channels, 3 * channels), BF16),
        ],
        compiler_params=params(24, grid=0),
        cost_estimate=cost(0, 0),
        name="inner",
    )(x, top, *front_parts)


def outer_call(bottom, middle, border, weight, cols, devices):
    n_frames, size, channels = middle.shape
    rows = size // LANE_COLS + 1
    tap = 2 * n_frames * LANE_COLS * channels * channels
    return pl.pallas_call(
        functools.partial(outer_kernel, cols=cols),
        in_specs=in_vmem(4),
        out_specs=in_vmem(3),
        scratch_shapes=[pltpu.VMEM((n_frames + 2, rows * LANE_COLS, channels), BF16)],
        out_shape=[
            pltpu.VMEM((n_frames, rows, channels // 128, LANE_COLS, 128), F32),
            jax.ShapeDtypeStruct((devices, 2, channels), F32),
            pltpu.VMEM((3 * channels, channels), BF16),
        ],
        compiler_params=params(24, grid=0),
        cost_estimate=cost(15 * tap, 10),
        name="outer",
    )(bottom, middle, border, weight)


def back_call(hidden, halo, temporal, all_stats, vectors, back_parts, cols):
    n_frames, rows = hidden.shape[:2]
    channels = halo.shape[2]
    parts = len(back_parts)
    piece = back_parts[0].shape
    many = BATCH if n_frames % BATCH == 0 else 1
    tap = 2 * n_frames * LANE_COLS * channels * channels
    half = LANE_COLS // 2
    return pl.pallas_call(
        functools.partial(back_kernel, parts=parts, cols=cols),
        in_specs=in_vmem(7 + parts),
        out_specs=pl.BlockSpec(memory_space=pltpu.VMEM),
        scratch_shapes=[
            pltpu.VMEM((piece[0], parts, piece[1], piece[2]), F32),
            pltpu.VMEM((9 * channels, channels), BF16),
            pltpu.VMEM((many, channels // 128, LANE_COLS, 128), F32),
            pltpu.VMEM((rows + 1, many, half, channels), BF16),
            pltpu.VMEM((rows + 1, many, half, channels), BF16),
        ],
        out_shape=jax.ShapeDtypeStruct((n_frames, rows // 2, cols // 2, channels), BF16),
        compiler_params=params(24, grid=0),
        cost_estimate=cost(12 * tap, 10, 4 << 20),
        name="back",
    )(hidden, halo, temporal, all_stats, *vectors, *back_parts)


def per_device(
    frames, spatial_weight, temporal_weight, down_weight, norm_gain, norm_shift, down_bias
):
    n_frames, rows, cols, channels = frames.shape
    row_devices, chan_devices = lax.axis_size("rows"), lax.axis_size("chan")
    part = spatial_weight.shape[0] // chan_devices
    split = part % 8 == 0 and chan_devices == 4 and row_devices == 8
    if split:
        first_cols, last_cols, taps, own = side_columns(
            frames, (spatial_weight, temporal_weight, down_weight), row_devices, part
        )
    else:
        first_cols, last_cols = side_columns(frames)
    right = shifted(first_cols, "chan", -1)
    left = shifted(last_cols, "chan", 1)
    if split:
        own = own.reshape(part, -1)
        pair = merged_call([own, swapped(own, "rows", 1)], 1)
    low_row, high_row, pack = extended_call(frames, left, right)
    if split:
        low_row, _ = lax.optimization_barrier((low_row, pair))
    top = shifted(low_row, "rows", 1)

    if split:
        taps = lax.all_to_all(taps, "rows", 0, 0)
        taps, _ = lax.optimization_barrier((taps, pack))
        taps = taps.reshape(channels, 3 * channels)
        over = swapped(taps, "chan", 2)
        beside = swapped(taps, "chan", 1)
        high_row, _ = lax.optimization_barrier((high_row, beside))
        bottom = shifted(high_row, "rows", -1)
        front_parts = [taps, beside, over, swapped(over, "chan", 1)]
        quads = [pair] + [swapped(pair, "rows", k) for k in (2, 4, 6)]
        quads, _ = lax.optimization_barrier((quads, over))
        own = merged_call(quads, 2).reshape(row_devices, part, -1)
    else:
        bottom = shifted(high_row, "rows", -1)
        joint = jnp.concatenate([spatial_weight, temporal_weight], 1)
        taps = lax.all_gather(joint, "rows", axis=0, tiled=True)
        width = 3 * channels
        front_parts = [taps[:, k * width : (k + 1) * width] for k in range(4)]
        own = lax.all_gather(down_weight, "rows", axis=0, tiled=True)

    x = build_call(frames, pack)
    top = masked_call(top)
    across = swapped(own, "chan", 2) if split else own
    first_row, middle, border, weight = inner_call(x, top, front_parts, split)
    halo = shifted(first_row, "rows", -1)
    if split:
        own, across, _ = lax.optimization_barrier((own, across, middle))
        back_parts = [own, swapped(own, "chan", 1), across, swapped(across, "chan", 1)]
    else:
        back_parts = [own.reshape(channels // 8, 8, -1)]
    hidden, stats, temporal = outer_call(
        bottom, middle, border, weight, cols, row_devices * chan_devices
    )
    stats, back_parts = lax.optimization_barrier((stats, back_parts))
    all_stats = lax.all_to_all(stats, ("rows", "chan"), 0, 0)
    vectors = [v.reshape(1, channels) for v in (norm_gain, norm_shift, down_bias)]
    return back_call(hidden, halo, temporal, all_stats, vectors, back_parts, cols)


def solution(mesh):
    placed = (
        P(None, "rows", "chan", None),
        P("rows", None),
        P("rows", None),
        P("rows", None),
        P(),
        P(),
        P(),
    )
    return jax.shard_map(
        per_device,
        mesh=mesh,
        in_specs=placed,
        out_specs=P(None, "rows", "chan", None),
        check_vma=False,
    )
```
